32 devices in a mesh: wide: 16 (over z, y, core), narrow: 2 (over x).
Axes of the slice: x: 2, y: 2, z: 4, core: 2. Of those that a mesh axis runs over, the one named last changes fastest.
Arguments:
- grid: bfloat16 [192, 256, 1440], P('wide', 'narrow'), may hold values from -6 to 6
- quad_weights: float32 [192], P('wide'), may hold values from 0.25 to 2
- orders: int32 [32], replicated, may hold values from 0 to 719, as said below
- legendre: bfloat16 [32, 720, 192], P('wide'), as said below
- mix_real: bfloat16 [256, 256], replicated, may hold values from -0.25 to 0.25
- mix_imag: bfloat16 [256, 256], replicated, may hold values from -0.25 to 0.25
- filter_gain: bfloat16 [720, 256], replicated, may hold values from 0.25 to 4
Outputs:
- field_out: bfloat16 [192, 256, 1440], P('wide', 'narrow')
The draws below stay inside these ranges and needn't reach their ends.
Inputs may be any that keep to these rules, and one draw needn't show every extreme that they name: `orders`: every order appears in one slot only; slots 2 q and 2 q + 1 hold p and 719 - p for some p below 360, so the 2 slots of a device come in such pairs. legendre[k, l, :] is zero for every degree l below orders[k].
All inputs are finite; a program needn't handle non-finite values.
Results may differ from the reference program's by a relative error of at most 0.007.
Values may be sent and summed in bfloat16 or wider, within the bound.
A program may use at most 64 MiB of HBM per device.

```python
import math
import jax
import jax.numpy as jnp
from jax import lax

NLON = 1440
L = 720
C = 256
LAT_DEV = 12
M = 32
NLAT = 192
N_WIDE = 16


def pair_orders(key):
    chosen = jax.random.permutation(key, L // 2)[:M // 2].astype(jnp.int32)
    position = jax.random.randint(jax.random.fold_in(key, 1), (), 0, M // 2)
    forced = chosen.at[position].set(0)
    half_pairs = jnp.where(jnp.any(chosen == 0), chosen, forced)
    return jnp.stack([half_pairs, L - 1 - half_pairs], axis=1).reshape(M)


def draw_orders(key, part):
    return pair_orders(jax.random.fold_in(key, 11))


def draw_legendre(key, part):
    order_slots = pair_orders(jax.random.fold_in(key, 11))
    value_key = jax.random.fold_in(key, 12)
    entries = jax.random.normal(value_key, (M, L, NLAT), jnp.float32)
    degree = jnp.arange(L, dtype=jnp.int32)[None, :, None]
    keep_mask = degree >= order_slots[:, None, None]
    return (jnp.where(keep_mask, entries, 0.0) * NLAT ** (-0.5)).astype(jnp.bfloat16)


def level_of(rng, dims, split, least, high):
    loudness, own = 1.0, jax.random.fold_in(rng, 6)
    for axis_at, blocks in split:
        steps = jnp.exp(jax.random.uniform(jax.random.fold_in(own, axis_at), (blocks,), jnp.float32, least / len(split), high / len(split)))
        loudness = loudness * jnp.repeat(steps, dims[axis_at] // blocks).reshape([-1 if axis == axis_at else 1 for axis in range(len(dims))])
    return loudness


def noise(stream_key, extent, width, reach, cuts=(), kind=jnp.bfloat16):
    level = level_of(stream_key, extent, cuts, -0.22, 0.18) if cuts else 1.0
    values = jax.random.normal(stream_key, extent, jnp.float32) * width * level
    return jnp.minimum(jnp.maximum(values, -reach), reach).astype(kind)


def setup_inputs(seed: int = 0) -> dict:
    keys = jax.random.split(jax.random.key(seed), 8)
    return {
        "grid": noise(keys[0], (NLAT, C, NLON), 1.0, 6.0, ((0, 16), (1, 2))),
        "quad_weights": jnp.clip(jnp.exp(math.log(2.0) - 2.0794415 * jax.random.uniform(keys[1], (NLAT,), jnp.float32) ** level_of(keys[1], (NLAT,), ((0, 16),), -0.2, 0.2)), 0.25, 2.0),
        "orders": draw_orders(jax.random.fold_in(keys[7], 71), 0),
        "legendre": draw_legendre(jax.random.fold_in(keys[7], 71), 0),
        "mix_real": noise(keys[4], (C, C), (2 * C) ** -0.5, 0.25),
        "mix_imag": noise(keys[5], (C, C), (2 * C) ** -0.5, 0.25),
        "filter_gain": jnp.clip(jnp.exp(jax.random.uniform(keys[6], (L, C), jnp.float32, math.log(0.25), math.log(4.0))), 0.25, 4.0).astype(jnp.bfloat16),
    }


highest = lax.Precision.HIGHEST

def fourier_tables(orders, lon_count):
    columns = jnp.arange(lon_count, dtype=jnp.int32)
    phase_int = orders.astype(jnp.int32)[:, None] * columns[None, :] % lon_count
    angles = phase_int.astype(jnp.float32) * (2.0 * math.pi / lon_count)
    return (jnp.cos(angles).astype(jnp.bfloat16), jnp.sin(angles).astype(jnp.bfloat16))

def reference(grid, quad_weights, orders, legendre, mix_real, mix_imag, filter_gain):
    cosine_low, sine_low = fourier_tables(orders, NLON)
    cosine_table = cosine_low.astype(jnp.float32)
    sine_table = sine_low.astype(jnp.float32)
    factor = 1.0 / math.sqrt(NLON)

    def forward(lat_block):
        lat_rows, weights = lat_block
        values = lat_rows.astype(jnp.float32)
        real_part = jnp.einsum('acn,kn->kac', values, cosine_table, precision=highest) * factor
        imag_part = -jnp.einsum('acn,kn->kac', values, sine_table, precision=highest) * factor
        spectra = jnp.stack([real_part, imag_part], axis=2) * weights[None, :, None, None]
        return spectra.astype(jnp.bfloat16)
    blocks = lax.map(forward, (grid.reshape(N_WIDE, LAT_DEV, C, NLON), quad_weights.reshape(N_WIDE, LAT_DEV)))
    spectra = jnp.transpose(blocks, (1, 0, 2, 3, 4)).reshape(M, NLAT, 2 * C)
    legendre_f = legendre.astype(jnp.float32)
    coeffs = jnp.einsum('mlx,mxk->mlk', legendre_f, spectra.astype(jnp.float32)).astype(jnp.bfloat16)
    coeffs = coeffs.reshape(M * L, 2, C)
    real_in = coeffs[:, 0]
    imag_in = coeffs[:, 1]
    mixed_real = jnp.dot(real_in, mix_real, preferred_element_type=jnp.float32) - jnp.dot(imag_in, mix_imag, preferred_element_type=jnp.float32)
    mixed_imag = jnp.dot(real_in, mix_imag, preferred_element_type=jnp.float32) + jnp.dot(imag_in, mix_real, preferred_element_type=jnp.float32)
    gain_rows = jnp.tile(filter_gain.astype(jnp.float32), (M, 1))
    mixed_coeffs = jnp.stack([mixed_real * gain_rows, mixed_imag * gain_rows], axis=1).astype(jnp.bfloat16)
    mixed_coeffs = mixed_coeffs.reshape(M, L, 2 * C)
    synthesis = jnp.einsum('mlx,mlk->mxk', legendre_f, mixed_coeffs.astype(jnp.float32)).astype(jnp.bfloat16)
    synthesis = jnp.transpose(synthesis.reshape(M, N_WIDE, LAT_DEV, 2, C), (1, 0, 2, 3, 4))

    def inverse(lat_block):
        values = lat_block.astype(jnp.float32)
        field_out = jnp.einsum('kac,kn->acn', values[:, :, 0], cosine_table, precision=highest)
        field_out = field_out - jnp.einsum('kac,kn->acn', values[:, :, 1], sine_table, precision=highest)
        return (field_out / math.sqrt(M)).astype(jnp.bfloat16)
    result = lax.map(inverse, synthesis)
    return result.reshape(NLAT, C, NLON)
```

```python
import functools
import math

import jax
import jax.numpy as jnp
from jax import lax
from jax.experimental import pallas as pl
from jax.experimental.pallas import tpu as pltpu
from jax.sharding import PartitionSpec as P

MESH = pl.DeviceIdType.MESH
SUB = 8
LANES = 128


def fourier_tables(orders, lon_count):
    columns = jnp.arange(lon_count, dtype=jnp.int32)
    phase_int = orders[:, None] * columns[None, :] % lon_count
    angles = phase_int.astype(jnp.float32) * (2.0 * math.pi / lon_count)
    return (jnp.cos(angles).astype(jnp.bfloat16), jnp.sin(angles).astype(jnp.bfloat16))


def general_shards(grid, quad_weights, orders, legendre, mix_real, mix_imag, filter_gain):
    lon_count = grid.shape[2]
    order_count = orders.shape[0]
    cosine_table, sine_table = fourier_tables(orders, lon_count)
    factor = 1.0 / math.sqrt(lon_count)
    real_part = (
        jnp.einsum("acn,kn->kac", grid, cosine_table, preferred_element_type=jnp.float32) * factor
    )
    imag_part = (
        -jnp.einsum("acn,kn->kac", grid, sine_table, preferred_element_type=jnp.float32) * factor
    )
    spectra = (
        jnp.stack([real_part, imag_part], axis=2) * quad_weights[None, :, None, None]
    ).astype(jnp.bfloat16)
    by_order = lax.all_to_all(spectra, "wide", split_axis=0, concat_axis=1, tiled=True)
    m_dev = by_order.shape[0]
    lat_count = by_order.shape[1]
    chan_dev = by_order.shape[3]
    deg_count = legendre.shape[1]
    coeffs = jnp.einsum(
        "mlx,mxk->mlk",
        legendre,
        by_order.reshape(m_dev, lat_count, 2 * chan_dev),
        preferred_element_type=jnp.float32,
    )
    coeffs = coeffs.astype(jnp.bfloat16).reshape(m_dev, deg_count, 2, chan_dev)
    deg_dev = deg_count // lax.axis_size("narrow")
    gain_rows = lax.dynamic_slice_in_dim(
        filter_gain, lax.axis_index("narrow") * deg_dev, deg_dev, 0
    ).astype(jnp.float32)
    upper = jnp.concatenate([mix_real, mix_imag], axis=1)
    lower = jnp.concatenate([-mix_imag, mix_real], axis=1)
    wide_block = jnp.concatenate([upper, lower], axis=0)
    fragment = lax.all_to_all(coeffs, "narrow", split_axis=1, concat_axis=3, tiled=True)
    frag_count = fragment.shape[0]
    chan_all = fragment.shape[3]
    flat_rows = fragment.reshape(frag_count * deg_dev, 2 * chan_all)
    product = jnp.dot(flat_rows, wide_block, preferred_element_type=jnp.float32)
    product = product.reshape(frag_count, deg_dev, 2, chan_all) * gain_rows[None, :, None, :]
    mixed_coeffs = product.astype(jnp.bfloat16)
    back_coeffs = lax.all_to_all(mixed_coeffs, "narrow", split_axis=3, concat_axis=1, tiled=True)
    synthesis = jnp.einsum(
        "mlx,mlk->mxk",
        legendre,
        back_coeffs.reshape(m_dev, deg_count, 2 * chan_dev),
        preferred_element_type=jnp.float32,
    )
    synthesis = synthesis.astype(jnp.bfloat16).reshape(m_dev, lat_count, 2, chan_dev)
    by_latitude = lax.all_to_all(synthesis, "wide", split_axis=1, concat_axis=0, tiled=True)
    field_out = jnp.einsum(
        "kac,kn->acn", by_latitude[:, :, 0], cosine_table, preferred_element_type=jnp.float32
    )
    field_out = field_out - jnp.einsum(
        "kac,kn->acn", by_latitude[:, :, 1], sine_table, preferred_element_type=jnp.float32
    )
    return (field_out / math.sqrt(order_count)).astype(jnp.bfloat16)


def turn_cosine(phase, period):
    quarter = period // 4
    turns = jnp.floor(phase * (1.0 / quarter) + 0.5)
    angle = (phase - turns * quarter) * (2.0 * math.pi / period)
    quadrant = turns - 4.0 * jnp.floor(turns * 0.25)
    sq = angle * angle
    cosine = 1.0 + sq * (-0.5 + sq * (1.0 / 24 + sq * (-1.0 / 720 + sq * (1.0 / 40320))))
    sine = angle * (1.0 + sq * (-1.0 / 6 + sq * (1.0 / 120 + sq * (-1.0 / 5040 + sq * (1.0 / 362880)))))
    odd = (quadrant == 1.0) | (quadrant == 3.0)
    flip = (quadrant == 1.0) | (quadrant == 2.0)
    value = jnp.where(odd, sine, cosine)
    return jnp.where(flip, -value, value)


def spectral_kernel(
    dims, orders_ref, quad_ref, grid_hbm, leg_hbm, mixr_hbm, mixi_hbm, gain_hbm,
    out_ref, tabt_ref,
    grid_v, leg_v, mixr_v, mixi_v, gain_v, tab, spread_a, spread_b, send1, recv1, lt, lf,
    weight, mixed, send2, recv2, flat2,
    grid_sem, in_sem, local_sem, s_send, s_recv, f_send, f_recv, b_send, b_recv,
):
    n_wide, lat_dev, lon_count, chan, m_dev, deg_count = dims
    order_count = n_wide * m_dev
    rows = 2 * order_count
    rest = lat_dev - SUB
    parts = m_dev + 1
    half = n_wide * SUB
    pairs = lat_dev // 2
    me = lax.axis_index("wide")
    x = lax.axis_index("narrow")
    partner = 1 - x

    grid_copies = []
    for p in range(pairs):
        copy = pltpu.make_async_copy(
            grid_hbm.at[pl.ds(2 * p, 2)], grid_v.at[pl.ds(2 * p, 2)], grid_sem.at[p]
        )
        copy.start()
        grid_copies.append(copy)
    in_copies = []
    for i, (src, dst) in enumerate(
        ((leg_hbm, leg_v), (mixr_hbm, mixr_v), (mixi_hbm, mixi_v), (gain_hbm, gain_v))
    ):
        copy = pltpu.make_async_copy(src, dst, in_sem.at[i])
        copy.start()
        in_copies.append(copy)

    barrier = pltpu.get_barrier_semaphore()
    for d in range(1, n_wide):
        pl.semaphore_signal(
            barrier, inc=1, device_id=((me + d) % n_wide, x), device_id_type=MESH
        )
    pl.semaphore_signal(barrier, inc=1, device_id=(me, partner), device_id_type=MESH)

    row = lax.broadcasted_iota(jnp.int32, (rows, LANES), 0)
    lane = lax.broadcasted_iota(jnp.int32, (rows, LANES), 1)
    block_rows = 2 * n_wide
    order_row = jnp.zeros((rows, LANES), jnp.int32)
    for j in range(m_dev):
        for w in range(n_wide):
            slot = orders_ref[w * m_dev + j]
            hit = (row == j * block_rows + w) | (row == j * block_rows + n_wide + w)
            order_row = jnp.where(hit, slot, order_row)
    shift = jnp.zeros((rows, LANES), jnp.int32)
    for j in range(m_dev):
        low = j * block_rows + n_wide
        shift = jnp.where((row >= low) & (row < low + n_wide), lon_count // 4, shift)
    for start in range(0, lon_count, LANES):
        size = min(LANES, lon_count - start)
        phase = (order_row * (lane + start) + shift).astype(jnp.float32)
        value = turn_cosine(phase, lon_count)
        tab[:, start:start + size] = value.astype(jnp.bfloat16)[:, :size]
        tabt_ref[start:start + size, :] = jnp.transpose(value)[:size].astype(jnp.bfloat16)

    factor = 1.0 / math.sqrt(lon_count)

    def transform(p):
        grid_copies[p].wait()
        rhs = jnp.concatenate([grid_v[2 * p], grid_v[2 * p + 1]], axis=1)
        res = jnp.dot(tab[...], rhs, preferred_element_type=jnp.float32)
        for i in range(2):
            a = 2 * p + i
            part = res[:, i * chan:(i + 1) * chan] * (quad_ref[a] * factor)
            if a < SUB:
                spread_a[a * rows:(a + 1) * rows, :] = part
            else:
                for j in range(m_dev):
                    at = (j * rest + a - SUB) * block_rows
                    spread_b[at:at + block_rows, :] = part[j * block_rows:(j + 1) * block_rows]

    def wide_copy(part, d):
        to = (me + d) % n_wide
        where = pl.ds(0, m_dev) if part == 0 else pl.ds(m_dev, 1)
        return pltpu.make_async_remote_copy(
            src_ref=send1.at[to, where],
            dst_ref=recv1.at[0, me, where],
            send_sem=s_send.at[part, d],
            recv_sem=s_recv.at[part, me],
            device_id=(to, x),
            device_id_type=MESH,
        )

    def wide_arrival(part, src):
        where = pl.ds(0, m_dev) if part == 0 else pl.ds(m_dev, 1)
        return pltpu.make_async_remote_copy(
            src_ref=send1.at[src, where],
            dst_ref=recv1.at[0, src, where],
            send_sem=s_send.at[part, 0],
            recv_sem=s_recv.at[part, src],
            device_id=(src, x),
            device_id_type=MESH,
        )

    def forward_copy(part, src):
        where = pl.ds(0, m_dev) if part == 0 else pl.ds(m_dev, 1)
        return pltpu.make_async_remote_copy(
            src_ref=recv1.at[0, src, where],
            dst_ref=recv1.at[1, src, where],
            send_sem=f_send.at[part, src],
            recv_sem=f_recv.at[part, src],
            device_id=(me, partner),
            device_id_type=MESH,
        )

    def own_copy(part):
        where = pl.ds(0, m_dev) if part == 0 else pl.ds(m_dev, 1)
        return pltpu.make_async_copy(
            send1.at[me, where], recv1.at[0, me, where], local_sem.at[part]
        )

    for p in range(SUB // 2):
        transform(p)
    for w in range(n_wide):
        for j in range(m_dev):
            for ri in range(2):
                at = j * block_rows + ri * n_wide + w
                send1[w, j, :, ri * chan:(ri + 1) * chan] = spread_a[
                    pl.ds(at, SUB, stride=rows), :
                ].astype(jnp.bfloat16)
    pl.semaphore_wait(barrier, n_wide)
    for d in range(1, n_wide):
        wide_copy(0, d).start()
    own_copy(0).start()

    for p in range(SUB // 2, pairs):
        transform(p)
    for w in range(n_wide):
        for ri in range(2):
            send1[w, m_dev, :, ri * chan:(ri + 1) * chan] = spread_b[
                pl.ds(ri * n_wide + w, SUB, stride=block_rows), :
            ].astype(jnp.bfloat16)
    for d in range(1, n_wide):
        wide_copy(1, d).start()
    own_copy(1).start()
    for part in range(2):
        own_copy(part).wait()
        forward_copy(part, me).start()

    for copy in in_copies:
        copy.wait()
    lat_count = n_wide * lat_dev
    slot = lax.broadcasted_iota(jnp.int32, (2 * half, lat_count), 0)
    lat = lax.broadcasted_iota(jnp.int32, (2 * half, lat_count), 1)
    local = slot % SUB
    device = jnp.where(slot < half, slot, slot - half) // SUB
    for j in range(m_dev):
        tail = jnp.where(
            (local >= j * rest) & (local < (j + 1) * rest),
            device * lat_dev + SUB + local - j * rest,
            -1,
        )
        want = jnp.where(slot < half, device * lat_dev + local, tail)
        pick = (want == lat).astype(jnp.bfloat16)
        moved = jnp.dot(pick, leg_v[j], preferred_element_type=jnp.float32)
        lt[j] = moved.astype(jnp.bfloat16)
        lf[j] = jnp.transpose(moved).astype(jnp.bfloat16)
    own_cols = pl.ds(pl.multiple_of(x * chan, chan), chan)
    for i, who in enumerate((x, partner)):
        in_rows = pl.ds(pl.multiple_of(who * chan, chan), chan)
        re = mixr_v[in_rows, own_cols]
        im = mixi_v[in_rows, own_cols]
        top = 2 * i * chan
        weight[top:top + chan, :chan] = re
        weight[top:top + chan, chan:] = im
        weight[top + chan:top + 2 * chan, :chan] = -im
        weight[top + chan:top + 2 * chan, chan:] = re

    for part in range(2):
        for d in range(1, n_wide):
            src = (me + n_wide - d) % n_wide
            wide_arrival(part, src).wait_recv()
            forward_copy(part, src).start()
    for part in range(2):
        for d in range(n_wide):
            forward_copy(part, (me + n_wide - d) % n_wide).wait_recv()

    gain = gain_v[:, own_cols].astype(jnp.float32)
    gain = jnp.concatenate([gain, gain], axis=1)
    tails = []
    for j in range(m_dev):
        sides = []
        for side in range(2):
            head = recv1[side, :, j].reshape(half, 2 * chan)
            tail = recv1[side, :, m_dev].reshape(half, 2 * chan)
            sides.append(jnp.concatenate([head, tail], axis=0))
        spec = jnp.concatenate(sides, axis=1)
        coeffs = jnp.dot(lf[j], spec, preferred_element_type=jnp.float32).astype(jnp.bfloat16)
        product = jnp.dot(coeffs, weight[...], preferred_element_type=jnp.float32)
        mixed[j] = (product * gain).astype(jnp.bfloat16)
        syn = jnp.dot(lt[j], mixed[j], preferred_element_type=jnp.float32)
        send2[:, j] = syn[:half].astype(jnp.bfloat16).reshape(n_wide, SUB, 2 * chan)
        tails.append(syn[half:])
    total = functools.reduce(lambda a, b: a + b, tails)
    send2[:, m_dev] = total.astype(jnp.bfloat16).reshape(n_wide, SUB, 2 * chan)

    def back_copy(to, d):
        return pltpu.make_async_remote_copy(
            src_ref=send2.at[to],
            dst_ref=recv2.at[me],
            send_sem=b_send.at[d],
            recv_sem=b_recv.at[me],
            device_id=(to, x),
            device_id_type=MESH,
        )

    def back_arrival(src):
        return pltpu.make_async_remote_copy(
            src_ref=send2.at[src],
            dst_ref=recv2.at[src],
            send_sem=b_send.at[0],
            recv_sem=b_recv.at[src],
            device_id=(src, x),
            device_id_type=MESH,
        )

    for d in range(1, n_wide):
        back_copy((me + d) % n_wide, d).start()
    own_back = pltpu.make_async_copy(send2.at[me], recv2.at[me], local_sem.at[2])
    own_back.start()
    for part in range(2):
        for d in range(1, n_wide):
            wide_copy(part, d).wait_send()
        for d in range(n_wide):
            forward_copy(part, (me + n_wide - d) % n_wide).wait_send()
    own_back.wait()
    for d in range(1, n_wide):
        back_arrival((me + n_wide - d) % n_wide).wait_recv()
    for ri in range(2):
        flat2[ri] = recv2[:, :, :, ri * chan:(ri + 1) * chan].astype(jnp.float32).reshape(
            n_wide * parts * SUB, chan
        )
    for a in range(lat_dev):
        for j in range(m_dev):
            for ri in range(2):
                at = j * SUB + a if a < SUB else m_dev * SUB + j * rest + a - SUB
                top = j * block_rows + ri * n_wide
                out_ref[a, top:top + n_wide, :] = flat2[
                    ri, pl.ds(at, n_wide, stride=parts * SUB), :
                ].astype(jnp.bfloat16)
    for d in range(1, n_wide):
        back_copy((me + d) % n_wide, d).wait_send()


def field_kernel(scale, chan, tabt_ref, syn_ref, out_ref):
    rhs = jnp.concatenate([syn_ref[0], syn_ref[1]], axis=1)
    res = jnp.dot(tabt_ref[...], rhs, preferred_element_type=jnp.float32) * scale
    res = res.astype(jnp.bfloat16)
    out_ref[0] = res[:, :chan]
    out_ref[1] = res[:, chan:]


def fast_shards(grid, quad_weights, orders, legendre, mix_real, mix_imag, filter_gain):
    lat_dev, chan, lon_count = grid.shape
    order_count = orders.shape[0]
    m_dev, deg_count, lat_count = legendre.shape
    n_wide = lax.axis_size("wide")
    rows = 2 * order_count
    parts = m_dev + 1
    half = n_wide * SUB
    bf16, f32 = jnp.bfloat16, jnp.float32
    vmem = pl.BlockSpec(memory_space=pltpu.VMEM)
    smem = pl.BlockSpec(memory_space=pltpu.SMEM)
    hbm = pl.BlockSpec(memory_space=pl.ANY)
    dims = (n_wide, lat_dev, lon_count, chan, m_dev, deg_count)
    chan_all = mix_real.shape[0]
    dma = pltpu.SemaphoreType.DMA
    synthesis, table = pl.pallas_call(
        functools.partial(spectral_kernel, dims),
        out_shape=(
            jax.ShapeDtypeStruct((lat_dev, rows, chan), bf16),
            jax.ShapeDtypeStruct((lon_count, rows), bf16),
        ),
        in_specs=[smem, smem, hbm, hbm, hbm, hbm, hbm],
        out_specs=(vmem, vmem),
        scratch_shapes=[
            pltpu.VMEM((lat_dev, lon_count, chan), bf16),
            pltpu.VMEM((m_dev, lat_count, deg_count), bf16),
            pltpu.VMEM((chan_all, chan_all), bf16),
            pltpu.VMEM((chan_all, chan_all), bf16),
            pltpu.VMEM((deg_count, chan_all), bf16),
            pltpu.VMEM((rows, lon_count), bf16),
            pltpu.VMEM((SUB * rows, chan), f32),
            pltpu.VMEM(((lat_dev - SUB) * rows, chan), f32),
            pltpu.VMEM((n_wide, parts, SUB, 2 * chan), bf16),
            pltpu.VMEM((2, n_wide, parts, SUB, 2 * chan), bf16),
            pltpu.VMEM((m_dev, 2 * half, deg_count), bf16),
            pltpu.VMEM((m_dev, deg_count, 2 * half), bf16),
            pltpu.VMEM((4 * chan, 2 * chan), bf16),
            pltpu.VMEM((m_dev, deg_count, 2 * chan), bf16),
            pltpu.VMEM((n_wide, parts, SUB, 2 * chan), bf16),
            pltpu.VMEM((n_wide, parts, SUB, 2 * chan), bf16),
            pltpu.VMEM((2, n_wide * parts * SUB, chan), f32),
            dma((lat_dev // 2,)),
            dma((4,)),
            dma((3,)),
            dma((2, n_wide)),
            dma((2, n_wide)),
            dma((2, n_wide)),
            dma((2, n_wide)),
            dma((n_wide,)),
            dma((n_wide,)),
        ],
        compiler_params=pltpu.CompilerParams(
            collective_id=0, has_side_effects=True, vmem_limit_bytes=40 * 2**20
        ),
        name="spectral",
    )(
        orders, quad_weights, jnp.transpose(grid, (0, 2, 1)), jnp.transpose(legendre, (0, 2, 1)),
        mix_real, mix_imag, filter_gain,
    )
    field = pl.pallas_call(
        functools.partial(field_kernel, 1.0 / math.sqrt(order_count), chan),
        grid=(lat_dev // 2,),
        out_shape=jax.ShapeDtypeStruct((lat_dev, lon_count, chan), bf16),
        in_specs=[
            pl.BlockSpec((lon_count, rows), lambda p: (0, 0)),
            pl.BlockSpec((2, rows, chan), lambda p: (p, 0, 0)),
        ],
        out_specs=pl.BlockSpec((2, lon_count, chan), lambda p: (p, 0, 0)),
        name="field",
    )(table, synthesis)
    return jnp.transpose(field, (0, 2, 1))


def shards(grid, quad_weights, orders, legendre, mix_real, mix_imag, filter_gain):
    lat_dev, chan, lon_count = grid.shape
    m_dev = legendre.shape[0]
    n_wide = lax.axis_size("wide")
    rest = lat_dev - SUB
    fits = (
        lax.axis_size("narrow") == 2
        and chan == LANES
        and lon_count % 4 == 0
        and rest > 0
        and rest * m_dev == SUB
        and lat_dev % 2 == 0
        and n_wide % 16 == 0
        and lon_count * lon_count < 2**24
    )
    body = fast_shards if fits else general_shards
    return body(grid, quad_weights, orders, legendre, mix_real, mix_imag, filter_gain)


def solution(mesh):
    placed = (P("wide", "narrow", None), P("wide"), P(), P("wide", None, None), P(), P(), P())
    return jax.shard_map(
        shards, mesh=mesh, in_specs=placed, out_specs=P("wide", "narrow", None), check_vma=False
    )
```

```python
import functools
import math

import jax
import jax.numpy as jnp
from jax import lax
from jax.experimental import pallas as pl
from jax.experimental.pallas import tpu as pltpu
from jax.sharding import PartitionSpec as P

MESH = pl.DeviceIdType.MESH
SUB = 8
LANES = 128


def fourier_tables(orders, lon_count):
    columns = jnp.arange(lon_count, dtype=jnp.int32)
    phase_int = orders[:, None] * columns[None, :] % lon_count
    angles = phase_int.astype(jnp.float32) * (2.0 * math.pi / lon_count)
    return (jnp.cos(angles).astype(jnp.bfloat16), jnp.sin(angles).astype(jnp.bfloat16))


def general_shards(grid, quad_weights, orders, legendre, mix_real, mix_imag, filter_gain):
    lon_count = grid.shape[2]
    order_count = orders.shape[0]
    cosine_table, sine_table = fourier_tables(orders, lon_count)
    factor = 1.0 / math.sqrt(lon_count)
    real_part = (
        jnp.einsum("acn,kn->kac", grid, cosine_table, preferred_element_type=jnp.float32) * factor
    )
    imag_part = (
        -jnp.einsum("acn,kn->kac", grid, sine_table, preferred_element_type=jnp.float32) * factor
    )
    spectra = (
        jnp.stack([real_part, imag_part], axis=2) * quad_weights[None, :, None, None]
    ).astype(jnp.bfloat16)
    by_order = lax.all_to_all(spectra, "wide", split_axis=0, concat_axis=1, tiled=True)
    m_dev = by_order.shape[0]
    lat_count = by_order.shape[1]
    chan_dev = by_order.shape[3]
    deg_count = legendre.shape[1]
    coeffs = jnp.einsum(
        "mlx,mxk->mlk",
        legendre,
        by_order.reshape(m_dev, lat_count, 2 * chan_dev),
        preferred_element_type=jnp.float32,
    )
    coeffs = coeffs.astype(jnp.bfloat16).reshape(m_dev, deg_count, 2, chan_dev)
    deg_dev = deg_count // lax.axis_size("narrow")
    gain_rows = lax.dynamic_slice_in_dim(
        filter_gain, lax.axis_index("narrow") * deg_dev, deg_dev, 0
    ).astype(jnp.float32)
    upper = jnp.concatenate([mix_real, mix_imag], axis=1)
    lower = jnp.concatenate([-mix_imag, mix_real], axis=1)
    wide_block = jnp.concatenate([upper, lower], axis=0)
    fragment = lax.all_to_all(coeffs, "narrow", split_axis=1, concat_axis=3, tiled=True)
    frag_count = fragment.shape[0]
    chan_all = fragment.shape[3]
    flat_rows = fragment.reshape(frag_count * deg_dev, 2 * chan_all)
    product = jnp.dot(flat_rows, wide_block, preferred_element_type=jnp.float32)
    product = product.reshape(frag_count, deg_dev, 2, chan_all) * gain_rows[None, :, None, :]
    mixed_coeffs = product.astype(jnp.bfloat16)
    back_coeffs = lax.all_to_all(mixed_coeffs, "narrow", split_axis=3, concat_axis=1, tiled=True)
    synthesis = jnp.einsum(
        "mlx,mlk->mxk",
        legendre,
        back_coeffs.reshape(m_dev, deg_count, 2 * chan_dev),
        preferred_element_type=jnp.float32,
    )
    synthesis = synthesis.astype(jnp.bfloat16).reshape(m_dev, lat_count, 2, chan_dev)
    by_latitude = lax.all_to_all(synthesis, "wide", split_axis=1, concat_axis=0, tiled=True)
    field_out = jnp.einsum(
        "kac,kn->acn", by_latitude[:, :, 0], cosine_table, preferred_element_type=jnp.float32
    )
    field_out = field_out - jnp.einsum(
        "kac,kn->acn", by_latitude[:, :, 1], sine_table, preferred_element_type=jnp.float32
    )
    return (field_out / math.sqrt(order_count)).astype(jnp.bfloat16)


def turn_cosine(phase, period):
    quarter = period // 4
    turns = jnp.floor(phase * (1.0 / quarter) + 0.5)
    angle = (phase - turns * quarter) * (2.0 * math.pi / period)
    quadrant = turns - 4.0 * jnp.floor(turns * 0.25)
    sq = angle * angle
    cosine = 1.0 + sq * (-0.5 + sq * (1.0 / 24 + sq * (-1.0 / 720 + sq * (1.0 / 40320))))
    sine = angle * (1.0 + sq * (-1.0 / 6 + sq * (1.0 / 120 + sq * (-1.0 / 5040 + sq * (1.0 / 362880)))))
    odd = (quadrant == 1.0) | (quadrant == 3.0)
    flip = (quadrant == 1.0) | (quadrant == 2.0)
    value = jnp.where(odd, sine, cosine)
    return jnp.where(flip, -value, value)


def spectral_kernel(
    dims, orders_hbm, quad_hbm, grid_hbm, leg_hbm, mixr_hbm, mixi_hbm, gain_hbm,
    out_ref, tabt_ref,
    grid_v, leg_v, mixr_v, mixi_v, gain_v, tab, spread_a, spread_b, send1, recv1, lt, lf,
    weight, mixed, send2, recv2, flat2, orders_ref, quad_ref,
    grid_sem, in_sem, local_sem, s_send, s_recv, f_send, f_recv, b_send, b_recv,
):
    n_wide, lat_dev, lon_count, chan, m_dev, deg_count = dims
    order_count = n_wide * m_dev
    rows = 2 * order_count
    rest = lat_dev - SUB
    parts = m_dev + 1
    half = n_wide * SUB
    pairs = lat_dev // 2
    me = lax.axis_index("wide")
    x = lax.axis_index("narrow")
    partner = 1 - x

    scalar_copies = []
    for i, (src, dst) in enumerate(((orders_hbm, orders_ref), (quad_hbm, quad_ref))):
        copy = pltpu.make_async_copy(src, dst, in_sem.at[4 + i])
        copy.start()
        scalar_copies.append(copy)
    grid_copies = []
    for p in range(pairs):
        copy = pltpu.make_async_copy(
            grid_hbm.at[pl.ds(2 * p, 2)], grid_v.at[pl.ds(2 * p, 2)], grid_sem.at[p]
        )
        copy.start()
        grid_copies.append(copy)
    in_copies = []
    for i, (src, dst) in enumerate(
        ((leg_hbm, leg_v), (mixr_hbm, mixr_v), (mixi_hbm, mixi_v), (gain_hbm, gain_v))
    ):
        copy = pltpu.make_async_copy(src, dst, in_sem.at[i])
        copy.start()
        in_copies.append(copy)

    barrier = pltpu.get_barrier_semaphore()
    for d in range(1, n_wide):
        pl.semaphore_signal(
            barrier, inc=1, device_id=((me + d) % n_wide, x), device_id_type=MESH
        )
    pl.semaphore_signal(barrier, inc=1, device_id=(me, partner), device_id_type=MESH)

    for copy in scalar_copies:
        copy.wait()
    row = lax.broadcasted_iota(jnp.int32, (rows, LANES), 0)
    lane = lax.broadcasted_iota(jnp.int32, (rows, LANES), 1)
    block_rows = 2 * n_wide
    order_row = jnp.zeros((rows, LANES), jnp.int32)
    for j in range(m_dev):
        for w in range(n_wide):
            slot = orders_ref[w * m_dev + j]
            hit = (row == j * block_rows + w) | (row == j * block_rows + n_wide + w)
            order_row = jnp.where(hit, slot, order_row)
    shift = jnp.zeros((rows, LANES), jnp.int32)
    for j in range(m_dev):
        low = j * block_rows + n_wide
        shift = jnp.where((row >= low) & (row < low + n_wide), lon_count // 4, shift)
    for start in range(0, lon_count, LANES):
        size = min(LANES, lon_count - start)
        phase = (order_row * (lane + start) + shift).astype(jnp.float32)
        value = turn_cosine(phase, lon_count)
        tab[:, start:start + size] = value.astype(jnp.bfloat16)[:, :size]
        tabt_ref[start:start + size, :] = jnp.transpose(value)[:size].astype(jnp.bfloat16)

    factor = 1.0 / math.sqrt(lon_count)

    def transform(p):
        grid_copies[p].wait()
        rhs = jnp.concatenate([grid_v[2 * p], grid_v[2 * p + 1]], axis=1)
        res = jnp.dot(tab[...], rhs, preferred_element_type=jnp.float32)
        for i in range(2):
            a = 2 * p + i
            part = res[:, i * chan:(i + 1) * chan] * (quad_ref[a] * factor)
            if a < SUB:
                spread_a[a * rows:(a + 1) * rows, :] = part
            else:
                for j in range(m_dev):
                    at = (j * rest + a - SUB) * block_rows
                    spread_b[at:at + block_rows, :] = part[j * block_rows:(j + 1) * block_rows]

    def wide_copy(part, d):
        to = (me + d) % n_wide
        where = pl.ds(0, m_dev) if part == 0 else pl.ds(m_dev, 1)
        return pltpu.make_async_remote_copy(
            src_ref=send1.at[to, where],
            dst_ref=recv1.at[0, me, where],
            send_sem=s_send.at[part, d],
            recv_sem=s_recv.at[part, me],
            device_id=(to, x),
            device_id_type=MESH,
        )

    def wide_arrival(part, src):
        where = pl.ds(0, m_dev) if part == 0 else pl.ds(m_dev, 1)
        return pltpu.make_async_remote_copy(
            src_ref=send1.at[src, where],
            dst_ref=recv1.at[0, src, where],
            send_sem=s_send.at[part, 0],
            recv_sem=s_recv.at[part, src],
            device_id=(src, x),
            device_id_type=MESH,
        )

    def forward_copy(part, src):
        where = pl.ds(0, m_dev) if part == 0 else pl.ds(m_dev, 1)
        return pltpu.make_async_remote_copy(
            src_ref=recv1.at[0, src, where],
            dst_ref=recv1.at[1, src, where],
            send_sem=f_send.at[part, src],
            recv_sem=f_recv.at[part, src],
            device_id=(me, partner),
            device_id_type=MESH,
        )

    def own_copy(part):
        where = pl.ds(0, m_dev) if part == 0 else pl.ds(m_dev, 1)
        return pltpu.make_async_copy(
            send1.at[me, where], recv1.at[0, me, where], local_sem.at[part]
        )

    for p in range(SUB // 2):
        transform(p)
    for w in range(n_wide):
        for j in range(m_dev):
            for ri in range(2):
                at = j * block_rows + ri * n_wide + w
                send1[w, j, :, ri * chan:(ri + 1) * chan] = spread_a[
                    pl.ds(at, SUB, stride=rows), :
                ].astype(jnp.bfloat16)
    pl.semaphore_wait(barrier, n_wide)
    for d in range(1, n_wide):
        wide_copy(0, d).start()
    own_copy(0).start()

    for p in range(SUB // 2, pairs):
        transform(p)
    for w in range(n_wide):
        for ri in range(2):
            send1[w, m_dev, :, ri * chan:(ri + 1) * chan] = spread_b[
                pl.ds(ri * n_wide + w, SUB, stride=block_rows), :
            ].astype(jnp.bfloat16)
    for d in range(1, n_wide):
        wide_copy(1, d).start()
    own_copy(1).start()
    for part in range(2):
        own_copy(part).wait()
        forward_copy(part, me).start()

    for copy in in_copies:
        copy.wait()
    lat_count = n_wide * lat_dev
    slot = lax.broadcasted_iota(jnp.int32, (2 * half, lat_count), 0)
    lat = lax.broadcasted_iota(jnp.int32, (2 * half, lat_count), 1)
    local = slot % SUB
    device = jnp.where(slot < half, slot, slot - half) // SUB
    for j in range(m_dev):
        tail = jnp.where(
            (local >= j * rest) & (local < (j + 1) * rest),
            device * lat_dev + SUB + local - j * rest,
            -1,
        )
        want = jnp.where(slot < half, device * lat_dev + local, tail)
        pick = (want == lat).astype(jnp.bfloat16)
        moved = jnp.dot(pick, leg_v[j], preferred_element_type=jnp.float32)
        lt[j] = moved.astype(jnp.bfloat16)
        lf[j] = jnp.transpose(moved).astype(jnp.bfloat16)
    own_cols = pl.ds(pl.multiple_of(x * chan, chan), chan)
    for i, who in enumerate((x, partner)):
        in_rows = pl.ds(pl.multiple_of(who * chan, chan), chan)
        re = mixr_v[in_rows, own_cols]
        im = mixi_v[in_rows, own_cols]
        top = 2 * i * chan
        weight[top:top + chan, :chan] = re
        weight[top:top + chan, chan:] = im
        weight[top + chan:top + 2 * chan, :chan] = -im
        weight[top + chan:top + 2 * chan, chan:] = re

    for part in range(2):
        for d in range(1, n_wide):
            src = (me + n_wide - d) % n_wide
            wide_arrival(part, src).wait_recv()
            forward_copy(part, src).start()
    for part in range(2):
        for d in range(n_wide):
            forward_copy(part, (me + n_wide - d) % n_wide).wait_recv()

    gain = gain_v[:, own_cols].astype(jnp.float32)
    gain = jnp.concatenate([gain, gain], axis=1)
    tails = []
    for j in range(m_dev):
        sides = []
        for side in range(2):
            head = recv1[side, :, j].reshape(half, 2 * chan)
            tail = recv1[side, :, m_dev].reshape(half, 2 * chan)
            sides.append(jnp.concatenate([head, tail], axis=0))
        spec = jnp.concatenate(sides, axis=1)
        coeffs = jnp.dot(lf[j], spec, preferred_element_type=jnp.float32).astype(jnp.bfloat16)
        product = jnp.dot(coeffs, weight[...], preferred_element_type=jnp.float32)
        mixed[j] = (product * gain).astype(jnp.bfloat16)
        syn = jnp.dot(lt[j], mixed[j], preferred_element_type=jnp.float32)
        send2[:, j] = syn[:half].astype(jnp.bfloat16).reshape(n_wide, SUB, 2 * chan)
        tails.append(syn[half:])
    total = functools.reduce(lambda a, b: a + b, tails)
    send2[:, m_dev] = total.astype(jnp.bfloat16).reshape(n_wide, SUB, 2 * chan)

    def back_copy(to, d):
        return pltpu.make_async_remote_copy(
            src_ref=send2.at[to],
            dst_ref=recv2.at[me],
            send_sem=b_send.at[d],
            recv_sem=b_recv.at[me],
            device_id=(to, x),
            device_id_type=MESH,
        )

    def back_arrival(src):
        return pltpu.make_async_remote_copy(
            src_ref=send2.at[src],
            dst_ref=recv2.at[src],
            send_sem=b_send.at[0],
            recv_sem=b_recv.at[src],
            device_id=(src, x),
            device_id_type=MESH,
        )

    for d in range(1, n_wide):
        back_copy((me + d) % n_wide, d).start()
    own_back = pltpu.make_async_copy(send2.at[me], recv2.at[me], local_sem.at[2])
    own_back.start()
    for part in range(2):
        for d in range(1, n_wide):
            wide_copy(part, d).wait_send()
        for d in range(n_wide):
            forward_copy(part, (me + n_wide - d) % n_wide).wait_send()
    own_back.wait()
    for d in range(1, n_wide):
        back_arrival((me + n_wide - d) % n_wide).wait_recv()
    for ri in range(2):
        flat2[ri] = recv2[:, :, :, ri * chan:(ri + 1) * chan].astype(jnp.float32).reshape(
            n_wide * parts * SUB, chan
        )
    for a in range(lat_dev):
        for j in range(m_dev):
            for ri in range(2):
                at = j * SUB + a if a < SUB else m_dev * SUB + j * rest + a - SUB
                top = j * block_rows + ri * n_wide
                out_ref[a, top:top + n_wide, :] = flat2[
                    ri, pl.ds(at, n_wide, stride=parts * SUB), :
                ].astype(jnp.bfloat16)
    for d in range(1, n_wide):
        back_copy((me + d) % n_wide, d).wait_send()


def field_kernel(scale, chan, tabt_ref, syn_ref, out_ref):
    p = pl.program_id(0)
    rhs = jnp.concatenate([syn_ref[2 * p], syn_ref[2 * p + 1]], axis=1)
    res = jnp.dot(tabt_ref[...], rhs, preferred_element_type=jnp.float32) * scale
    res = res.astype(jnp.bfloat16)
    out_ref[0] = res[:, :chan]
    out_ref[1] = res[:, chan:]


def fast_shards(grid, quad_weights, orders, legendre, mix_real, mix_imag, filter_gain):
    lat_dev, chan, lon_count = grid.shape
    order_count = orders.shape[0]
    m_dev, deg_count, lat_count = legendre.shape
    n_wide = lax.axis_size("wide")
    rows = 2 * order_count
    parts = m_dev + 1
    half = n_wide * SUB
    bf16, f32 = jnp.bfloat16, jnp.float32
    vmem = pl.BlockSpec(memory_space=pltpu.VMEM)
    hbm = pl.BlockSpec(memory_space=pltpu.HBM)
    dims = (n_wide, lat_dev, lon_count, chan, m_dev, deg_count)
    chan_all = mix_real.shape[0]
    dma = pltpu.SemaphoreType.DMA
    synthesis, table = pl.pallas_call(
        functools.partial(spectral_kernel, dims),
        out_shape=(
            jax.ShapeDtypeStruct((lat_dev, rows, chan), bf16),
            jax.ShapeDtypeStruct((lon_count, rows), bf16),
        ),
        in_specs=[hbm] * 7,
        out_specs=(vmem, vmem),
        scratch_shapes=[
            pltpu.VMEM((lat_dev, lon_count, chan), bf16),
            pltpu.VMEM((m_dev, lat_count, deg_count), bf16),
            pltpu.VMEM((chan_all, chan_all), bf16),
            pltpu.VMEM((chan_all, chan_all), bf16),
            pltpu.VMEM((deg_count, chan_all), bf16),
            pltpu.VMEM((rows, lon_count), bf16),
            pltpu.VMEM((SUB * rows, chan), f32),
            pltpu.VMEM(((lat_dev - SUB) * rows, chan), f32),
            pltpu.VMEM((n_wide, parts, SUB, 2 * chan), bf16),
            pltpu.VMEM((2, n_wide, parts, SUB, 2 * chan), bf16),
            pltpu.VMEM((m_dev, 2 * half, deg_count), bf16),
            pltpu.VMEM((m_dev, deg_count, 2 * half), bf16),
            pltpu.VMEM((4 * chan, 2 * chan), bf16),
            pltpu.VMEM((m_dev, deg_count, 2 * chan), bf16),
            pltpu.VMEM((n_wide, parts, SUB, 2 * chan), bf16),
            pltpu.VMEM((n_wide, parts, SUB, 2 * chan), bf16),
            pltpu.VMEM((2, n_wide * parts * SUB, chan), f32),
            pltpu.SMEM((order_count,), jnp.int32),
            pltpu.SMEM((lat_dev,), f32),
            dma((lat_dev // 2,)),
            dma((6,)),
            dma((3,)),
            dma((2, n_wide)),
            dma((2, n_wide)),
            dma((2, n_wide)),
            dma((2, n_wide)),
            dma((n_wide,)),
            dma((n_wide,)),
        ],
        compiler_params=pltpu.CompilerParams(
            collective_id=0, has_side_effects=True, vmem_limit_bytes=40 * 2**20
        ),
        name="spectral",
    )(*(pltpu.with_memory_space_constraint(v, pltpu.HBM) for v in (
        orders, quad_weights, jnp.transpose(grid, (0, 2, 1)), jnp.transpose(legendre, (0, 2, 1)),
        mix_real, mix_imag, filter_gain,
    )))
    field = pl.pallas_call(
        functools.partial(field_kernel, 1.0 / math.sqrt(order_count), chan),
        grid=(lat_dev // 2,),
        out_shape=jax.ShapeDtypeStruct((lat_dev, lon_count, chan), bf16),
        in_specs=[vmem, vmem],
        out_specs=pl.BlockSpec((2, lon_count, chan), lambda p: (p, 0, 0)),
        compiler_params=pltpu.CompilerParams(vmem_limit_bytes=16 * 2**20),
        name="field",
    )(table, synthesis)
    return jnp.transpose(field, (0, 2, 1))


def shards(grid, quad_weights, orders, legendre, mix_real, mix_imag, filter_gain):
    lat_dev, chan, lon_count = grid.shape
    m_dev = legendre.shape[0]
    n_wide = lax.axis_size("wide")
    rest = lat_dev - SUB
    fits = (
        lax.axis_size("narrow") == 2
        and chan == LANES
        and lon_count % 4 == 0
        and rest > 0
        and rest * m_dev == SUB
        and lat_dev % 2 == 0
        and n_wide % 16 == 0
        and lon_count * lon_count < 2**24
    )
    body = fast_shards if fits else general_shards
    return body(grid, quad_weights, orders, legendre, mix_real, mix_imag, filter_gain)


def solution(mesh):
    placed = (P("wide", "narrow", None), P("wide"), P(), P("wide", None, None), P(), P(), P())
    return jax.shard_map(
        shards, mesh=mesh, in_specs=placed, out_specs=P("wide", "narrow", None), check_vma=False
    )
```

```python
import functools
import math

import jax
import jax.numpy as jnp
from jax import lax
from jax.experimental import pallas as pl
from jax.experimental.pallas import tpu as pltpu
from jax.sharding import PartitionSpec as P

MESH = pl.DeviceIdType.MESH
SUB = 8
LANES = 128


def fourier_tables(orders, lon_count):
    columns = jnp.arange(lon_count, dtype=jnp.int32)
    phase_int = orders[:, None] * columns[None, :] % lon_count
    angles = phase_int.astype(jnp.float32) * (2.0 * math.pi / lon_count)
    return (jnp.cos(angles).astype(jnp.bfloat16), jnp.sin(angles).astype(jnp.bfloat16))


def general_shards(grid, quad_weights, orders, legendre, mix_real, mix_imag, filter_gain):
    lon_count = grid.shape[2]
    order_count = orders.shape[0]
    cosine_table, sine_table = fourier_tables(orders, lon_count)
    factor = 1.0 / math.sqrt(lon_count)
    real_part = (
        jnp.einsum("acn,kn->kac", grid, cosine_table, preferred_element_type=jnp.float32) * factor
    )
    imag_part = (
        -jnp.einsum("acn,kn->kac", grid, sine_table, preferred_element_type=jnp.float32) * factor
    )
    spectra = (
        jnp.stack([real_part, imag_part], axis=2) * quad_weights[None, :, None, None]
    ).astype(jnp.bfloat16)
    by_order = lax.all_to_all(spectra, "wide", split_axis=0, concat_axis=1, tiled=True)
    m_dev = by_order.shape[0]
    lat_count = by_order.shape[1]
    chan_dev = by_order.shape[3]
    deg_count = legendre.shape[1]
    coeffs = jnp.einsum(
        "mlx,mxk->mlk",
        legendre,
        by_order.reshape(m_dev, lat_count, 2 * chan_dev),
        preferred_element_type=jnp.float32,
    )
    coeffs = coeffs.astype(jnp.bfloat16).reshape(m_dev, deg_count, 2, chan_dev)
    deg_dev = deg_count // lax.axis_size("narrow")
    gain_rows = lax.dynamic_slice_in_dim(
        filter_gain, lax.axis_index("narrow") * deg_dev, deg_dev, 0
    ).astype(jnp.float32)
    upper = jnp.concatenate([mix_real, mix_imag], axis=1)
    lower = jnp.concatenate([-mix_imag, mix_real], axis=1)
    wide_block = jnp.concatenate([upper, lower], axis=0)
    fragment = lax.all_to_all(coeffs, "narrow", split_axis=1, concat_axis=3, tiled=True)
    frag_count = fragment.shape[0]
    chan_all = fragment.shape[3]
    flat_rows = fragment.reshape(frag_count * deg_dev, 2 * chan_all)
    product = jnp.dot(flat_rows, wide_block, preferred_element_type=jnp.float32)
    product = product.reshape(frag_count, deg_dev, 2, chan_all) * gain_rows[None, :, None, :]
    mixed_coeffs = product.astype(jnp.bfloat16)
    back_coeffs = lax.all_to_all(mixed_coeffs, "narrow", split_axis=3, concat_axis=1, tiled=True)
    synthesis = jnp.einsum(
        "mlx,mlk->mxk",
        legendre,
        back_coeffs.reshape(m_dev, deg_count, 2 * chan_dev),
        preferred_element_type=jnp.float32,
    )
    synthesis = synthesis.astype(jnp.bfloat16).reshape(m_dev, lat_count, 2, chan_dev)
    by_latitude = lax.all_to_all(synthesis, "wide", split_axis=1, concat_axis=0, tiled=True)
    field_out = jnp.einsum(
        "kac,kn->acn", by_latitude[:, :, 0], cosine_table, preferred_element_type=jnp.float32
    )
    field_out = field_out - jnp.einsum(
        "kac,kn->acn", by_latitude[:, :, 1], sine_table, preferred_element_type=jnp.float32
    )
    return (field_out / math.sqrt(order_count)).astype(jnp.bfloat16)


def turn_cosine(phase, period):
    quarter = period // 4
    turns = jnp.floor(phase * (1.0 / quarter) + 0.5)
    angle = (phase - turns * quarter) * (2.0 * math.pi / period)
    quadrant = turns - 4.0 * jnp.floor(turns * 0.25)
    sq = angle * angle
    cosine = 1.0 + sq * (-0.5 + sq * (1.0 / 24 + sq * (-1.0 / 720 + sq * (1.0 / 40320))))
    sine = angle * (1.0 + sq * (-1.0 / 6 + sq * (1.0 / 120 + sq * (-1.0 / 5040 + sq * (1.0 / 362880)))))
    odd = (quadrant == 1.0) | (quadrant == 3.0)
    flip = (quadrant == 1.0) | (quadrant == 2.0)
    value = jnp.where(odd, sine, cosine)
    return jnp.where(flip, -value, value)


def spectral_kernel(
    dims, orders_hbm, quad_hbm, grid_hbm, leg_hbm, mixr_hbm, mixi_hbm, gain_hbm,
    out_ref, tabt_ref,
    grid_v, leg_v, mixr_v, mixi_v, gain_v, tab, spread_a, spread_b, send1, recv1, lt, lf,
    weight, coeffs, mixed, send2, recv2, flat2, orders_ref, quad_ref,
    grid_sem, in_sem, local_sem, s_send, s_recv, f_send, f_recv, b_send, b_recv,
):
    n_wide, lat_dev, lon_count, chan, m_dev, deg_count = dims
    order_count = n_wide * m_dev
    rows = 2 * order_count
    rest = lat_dev - SUB
    parts = m_dev + 1
    half = n_wide * SUB
    pairs = lat_dev // 2
    me = lax.axis_index("wide")
    x = lax.axis_index("narrow")
    partner = 1 - x

    scalar_copies = []
    for i, (src, dst) in enumerate(((orders_hbm, orders_ref), (quad_hbm, quad_ref))):
        copy = pltpu.make_async_copy(src, dst, in_sem.at[4 + i])
        copy.start()
        scalar_copies.append(copy)
    grid_copies = []
    for p in range(pairs):
        copy = pltpu.make_async_copy(
            grid_hbm.at[pl.ds(2 * p, 2)], grid_v.at[pl.ds(2 * p, 2)], grid_sem.at[p]
        )
        copy.start()
        grid_copies.append(copy)
    half_w = n_wide // 2
    base = (me // half_w) * half_w
    spot = me % half_w

    def near(i):
        return base + (spot + i) % half_w

    def far(i):
        return half_w - base + (spot + i) % half_w

    barrier = pltpu.get_barrier_semaphore()
    targets = [(far(i), x) for i in range(half_w)]
    targets += [(near(i), partner) for i in range(half_w)]
    targets += [(near(i), x) for i in range(1, half_w)]
    for target in targets:
        pl.semaphore_signal(barrier, inc=1, device_id=target, device_id_type=MESH)

    in_copies = []
    for i, (src, dst) in enumerate(
        ((leg_hbm, leg_v), (mixr_hbm, mixr_v), (mixi_hbm, mixi_v), (gain_hbm, gain_v))
    ):
        copy = pltpu.make_async_copy(src, dst, in_sem.at[i])
        copy.start()
        in_copies.append(copy)

    for copy in scalar_copies:
        copy.wait()
    row = lax.broadcasted_iota(jnp.int32, (rows, LANES), 0)
    lane = lax.broadcasted_iota(jnp.int32, (rows, LANES), 1)
    block_rows = 2 * n_wide
    order_row = jnp.zeros((rows, LANES), jnp.int32)
    for j in range(m_dev):
        for w in range(n_wide):
            slot = orders_ref[w * m_dev + j]
            hit = (row == j * block_rows + w) | (row == j * block_rows + n_wide + w)
            order_row = jnp.where(hit, slot, order_row)
    shift = jnp.zeros((rows, LANES), jnp.int32)
    for j in range(m_dev):
        low = j * block_rows + n_wide
        shift = jnp.where((row >= low) & (row < low + n_wide), lon_count // 4, shift)
    for start in range(0, lon_count, LANES):
        size = min(LANES, lon_count - start)
        phase = (order_row * (lane + start) + shift).astype(jnp.float32)
        value = turn_cosine(phase, lon_count)
        tab[:, start:start + size] = value.astype(jnp.bfloat16)[:, :size]
        tabt_ref[start:start + size, :] = jnp.transpose(value)[:size].astype(jnp.bfloat16)

    factor = 1.0 / math.sqrt(lon_count)

    def transform(p):
        grid_copies[p].wait()
        rhs = jnp.concatenate([grid_v[2 * p], grid_v[2 * p + 1]], axis=1)
        res = jnp.dot(tab[...], rhs, preferred_element_type=jnp.float32)
        for i in range(2):
            a = 2 * p + i
            part = res[:, i * chan:(i + 1) * chan] * (quad_ref[a] * factor)
            if a < SUB:
                spread_a[a * rows:(a + 1) * rows, :] = part
            else:
                for j in range(m_dev):
                    at = (j * rest + a - SUB) * block_rows
                    spread_b[at:at + block_rows, :] = part[j * block_rows:(j + 1) * block_rows]

    def span(part):
        return pl.ds(0, m_dev) if part == 0 else pl.ds(m_dev, 1)

    def wide_copy(part, to, sem):
        return pltpu.make_async_remote_copy(
            src_ref=send1.at[to, span(part)],
            dst_ref=recv1.at[0, me, span(part)],
            send_sem=s_send.at[part, sem],
            recv_sem=s_recv.at[part, me],
            device_id=(to, x),
            device_id_type=MESH,
        )

    def cross_copy(part, i):
        return pltpu.make_async_remote_copy(
            src_ref=send1.at[near(i), span(part)],
            dst_ref=recv1.at[1, me, span(part)],
            send_sem=f_send.at[part, i],
            recv_sem=f_recv.at[part, me],
            device_id=(near(i), partner),
            device_id_type=MESH,
        )

    def wide_arrival(part, src):
        return pltpu.make_async_remote_copy(
            src_ref=send1.at[src, span(part)],
            dst_ref=recv1.at[0, src, span(part)],
            send_sem=s_send.at[part, 0],
            recv_sem=s_recv.at[part, src],
            device_id=(src, x),
            device_id_type=MESH,
        )

    def forward_copy(part, i):
        return pltpu.make_async_remote_copy(
            src_ref=recv1.at[0, far(i), span(part)],
            dst_ref=recv1.at[1, far(i), span(part)],
            send_sem=f_send.at[part, half_w + i],
            recv_sem=f_recv.at[part, far(i)],
            device_id=(me, partner),
            device_id_type=MESH,
        )

    def partner_arrival(part, src):
        return pltpu.make_async_remote_copy(
            src_ref=recv1.at[0, src, span(part)],
            dst_ref=recv1.at[1, src, span(part)],
            send_sem=f_send.at[part, 0],
            recv_sem=f_recv.at[part, src],
            device_id=(me, partner),
            device_id_type=MESH,
        )

    def out_copies(part):
        copies = [wide_copy(part, far(i), i) for i in range(half_w)]
        copies += [cross_copy(part, i) for i in range(half_w)]
        copies += [wide_copy(part, near(i), half_w + i) for i in range(1, half_w)]
        return copies

    def own_copy(part):
        return pltpu.make_async_copy(
            send1.at[me, span(part)], recv1.at[0, me, span(part)], local_sem.at[part]
        )

    for p in range(SUB // 2):
        transform(p)
    for w in range(n_wide):
        for j in range(m_dev):
            for ri in range(2):
                at = j * block_rows + ri * n_wide + w
                send1[w, j, :, ri * chan:(ri + 1) * chan] = spread_a[
                    pl.ds(at, SUB, stride=rows), :
                ].astype(jnp.bfloat16)
    pl.semaphore_wait(barrier, len(targets))
    for copy in out_copies(0):
        copy.start()
    own_copy(0).start()

    for p in range(SUB // 2, pairs):
        transform(p)
    for w in range(n_wide):
        for ri in range(2):
            send1[w, m_dev, :, ri * chan:(ri + 1) * chan] = spread_b[
                pl.ds(ri * n_wide + w, SUB, stride=block_rows), :
            ].astype(jnp.bfloat16)
    for copy in out_copies(1):
        copy.start()
    own_copy(1).start()

    for copy in in_copies:
        copy.wait()
    lat_count = n_wide * lat_dev
    slot = lax.broadcasted_iota(jnp.int32, (2 * half, lat_count), 0)
    lat = lax.broadcasted_iota(jnp.int32, (2 * half, lat_count), 1)
    local = slot % SUB
    device = jnp.where(slot < half, slot, slot - half) // SUB
    for j in range(m_dev):
        tail = jnp.where(
            (local >= j * rest) & (local < (j + 1) * rest),
            device * lat_dev + SUB + local - j * rest,
            -1,
        )
        want = jnp.where(slot < half, device * lat_dev + local, tail)
        pick = (want == lat).astype(jnp.bfloat16)
        moved = jnp.dot(pick, leg_v[j], preferred_element_type=jnp.float32)
        lt[j] = moved.astype(jnp.bfloat16)
        lf[j] = jnp.transpose(moved).astype(jnp.bfloat16)
    own_cols = pl.ds(pl.multiple_of(x * chan, chan), chan)
    for i, who in enumerate((x, partner)):
        in_rows = pl.ds(pl.multiple_of(who * chan, chan), chan)
        re = mixr_v[in_rows, own_cols]
        im = mixi_v[in_rows, own_cols]
        top = 2 * i * chan
        weight[top:top + chan, :chan] = re
        weight[top:top + chan, chan:] = im
        weight[top + chan:top + 2 * chan, :chan] = -im
        weight[top + chan:top + 2 * chan, chan:] = re

    for part in range(2):
        for i in range(half_w):
            wide_arrival(part, far(i)).wait_recv()
            forward_copy(part, i).start()
    for part in range(2):
        own_copy(part).wait()
        for i in range(1, half_w):
            wide_arrival(part, near(i)).wait_recv()

    def transform_lat(side, j):
        head = recv1[side, :, j].reshape(half, 2 * chan)
        tail = recv1[side, :, m_dev].reshape(half, 2 * chan)
        spec = jnp.concatenate([head, tail], axis=0)
        res = jnp.dot(lf[j], spec, preferred_element_type=jnp.float32)
        coeffs[j, :, 2 * side * chan:2 * (side + 1) * chan] = res.astype(jnp.bfloat16)

    for j in range(m_dev):
        transform_lat(0, j)
    for part in range(2):
        for i in range(half_w):
            partner_arrival(part, near(i)).wait_recv()
        for i in range(half_w):
            partner_arrival(part, far(i)).wait_recv()

    gain = gain_v[:, own_cols].astype(jnp.float32)
    gain = jnp.concatenate([gain, gain], axis=1)

    def back_copy(part, to, sem):
        where = pl.ds(0, 1) if part == 0 else pl.ds(1, parts - 1)
        return pltpu.make_async_remote_copy(
            src_ref=send2.at[to, where],
            dst_ref=recv2.at[me, where],
            send_sem=b_send.at[part, sem],
            recv_sem=b_recv.at[part, me],
            device_id=(to, x),
            device_id_type=MESH,
        )

    def back_arrival(part, src):
        where = pl.ds(0, 1) if part == 0 else pl.ds(1, parts - 1)
        return pltpu.make_async_remote_copy(
            src_ref=send2.at[src, where],
            dst_ref=recv2.at[src, where],
            send_sem=b_send.at[part, 0],
            recv_sem=b_recv.at[part, src],
            device_id=(src, x),
            device_id_type=MESH,
        )

    def back_copies(part):
        copies = [back_copy(part, far(i), i) for i in range(half_w)]
        return copies + [back_copy(part, near(i), half_w + i) for i in range(1, half_w)]

    tails = []
    for j in range(m_dev):
        transform_lat(1, j)
        product = jnp.dot(coeffs[j], weight[...], preferred_element_type=jnp.float32)
        mixed[j] = (product * gain).astype(jnp.bfloat16)
        syn = jnp.dot(lt[j], mixed[j], preferred_element_type=jnp.float32)
        send2[:, j] = syn[:half].astype(jnp.bfloat16).reshape(n_wide, SUB, 2 * chan)
        tails.append(syn[half:])
        if j == 0:
            for copy in back_copies(0):
                copy.start()
    total = functools.reduce(lambda a, b: a + b, tails)
    send2[:, m_dev] = total.astype(jnp.bfloat16).reshape(n_wide, SUB, 2 * chan)
    for copy in back_copies(1):
        copy.start()

    stride = parts * SUB

    def widen(src, ref):
        at = pl.ds(pl.multiple_of(src * stride, SUB), stride)
        block = ref[src]
        for ri in range(2):
            flat2[ri, at, :] = block[:, :, ri * chan:(ri + 1) * chan].astype(
                jnp.float32
            ).reshape(stride, chan)

    widen(me, send2)
    for part in range(2):
        for copy in out_copies(part):
            copy.wait_send()
        for i in range(half_w):
            forward_copy(part, i).wait_send()
    for src in [near(i) for i in range(1, half_w)] + [far(i) for i in range(half_w)]:
        for part in range(2):
            back_arrival(part, src).wait_recv()
        widen(src, recv2)
    for a in range(lat_dev):
        for j in range(m_dev):
            for ri in range(2):
                at = j * SUB + a if a < SUB else m_dev * SUB + j * rest + a - SUB
                top = j * block_rows + ri * n_wide
                out_ref[a, top:top + n_wide, :] = flat2[
                    ri, pl.ds(at, n_wide, stride=stride), :
                ].astype(jnp.bfloat16)
    for part in range(2):
        for copy in back_copies(part):
            copy.wait_send()


def field_kernel(scale, chan, tabt_ref, syn_ref, out_ref):
    p = pl.program_id(0)
    count = out_ref.shape[1]
    lons = pl.ds(pl.multiple_of(pl.program_id(1) * count, 16), count)
    rhs = jnp.concatenate([syn_ref[2 * p], syn_ref[2 * p + 1]], axis=1)
    res = jnp.dot(tabt_ref[lons, :], rhs, preferred_element_type=jnp.float32) * scale
    res = res.astype(jnp.bfloat16)
    out_ref[0] = res[:, :chan]
    out_ref[1] = res[:, chan:]


def fast_shards(grid, quad_weights, orders, legendre, mix_real, mix_imag, filter_gain):
    lat_dev, chan, lon_count = grid.shape
    order_count = orders.shape[0]
    m_dev, deg_count, lat_count = legendre.shape
    n_wide = lax.axis_size("wide")
    rows = 2 * order_count
    parts = m_dev + 1
    half = n_wide * SUB
    bf16, f32 = jnp.bfloat16, jnp.float32
    vmem = pl.BlockSpec(memory_space=pltpu.VMEM)
    hbm = pl.BlockSpec(memory_space=pltpu.HBM)
    dims = (n_wide, lat_dev, lon_count, chan, m_dev, deg_count)
    chan_all = mix_real.shape[0]
    dma = pltpu.SemaphoreType.DMA
    synthesis, table = pl.pallas_call(
        functools.partial(spectral_kernel, dims),
        out_shape=(
            jax.ShapeDtypeStruct((lat_dev, rows, chan), bf16),
            jax.ShapeDtypeStruct((lon_count, rows), bf16),
        ),
        in_specs=[hbm] * 7,
        out_specs=(vmem, vmem),
        scratch_shapes=[
            pltpu.VMEM((lat_dev, lon_count, chan), bf16),
            pltpu.VMEM((m_dev, lat_count, deg_count), bf16),
            pltpu.VMEM((chan_all, chan_all), bf16),
            pltpu.VMEM((chan_all, chan_all), bf16),
            pltpu.VMEM((deg_count, chan_all), bf16),
            pltpu.VMEM((rows, lon_count), bf16),
            pltpu.VMEM((SUB * rows, chan), f32),
            pltpu.VMEM(((lat_dev - SUB) * rows, chan), f32),
            pltpu.VMEM((n_wide, parts, SUB, 2 * chan), bf16),
            pltpu.VMEM((2, n_wide, parts, SUB, 2 * chan), bf16),
            pltpu.VMEM((m_dev, 2 * half, deg_count), bf16),
            pltpu.VMEM((m_dev, deg_count, 2 * half), bf16),
            pltpu.VMEM((4 * chan, 2 * chan), bf16),
            pltpu.VMEM((m_dev, deg_count, 4 * chan), bf16),
            pltpu.VMEM((m_dev, deg_count, 2 * chan), bf16),
            pltpu.VMEM((n_wide, parts, SUB, 2 * chan), bf16),
            pltpu.VMEM((n_wide, parts, SUB, 2 * chan), bf16),
            pltpu.VMEM((2, n_wide * parts * SUB, chan), f32),
            pltpu.SMEM((order_count,), jnp.int32),
            pltpu.SMEM((lat_dev,), f32),
            dma((lat_dev // 2,)),
            dma((6,)),
            dma((2,)),
            dma((2, n_wide)),
            dma((2, n_wide)),
            dma((2, n_wide)),
            dma((2, n_wide)),
            dma((2, n_wide)),
            dma((2, n_wide)),
        ],
        compiler_params=pltpu.CompilerParams(
            collective_id=0, has_side_effects=True, vmem_limit_bytes=40 * 2**20
        ),
        name="spectral",
    )(*(pltpu.with_memory_space_constraint(v, pltpu.HBM) for v in (
        orders, quad_weights, jnp.transpose(grid, (0, 2, 1)), jnp.transpose(legendre, (0, 2, 1)),
        mix_real, mix_imag, filter_gain,
    )))
    field = pl.pallas_call(
        functools.partial(field_kernel, 1.0 / math.sqrt(order_count), chan),
        grid=(lat_dev // 2, 2),
        out_shape=jax.ShapeDtypeStruct((lat_dev, lon_count, chan), bf16),
        in_specs=[vmem, vmem],
        out_specs=pl.BlockSpec((2, lon_count // 2, chan), lambda p, h: (p, h, 0)),
        compiler_params=pltpu.CompilerParams(vmem_limit_bytes=16 * 2**20),
        name="field",
    )(table, synthesis)
    return jnp.transpose(field, (0, 2, 1))


def shards(grid, quad_weights, orders, legendre, mix_real, mix_imag, filter_gain):
    lat_dev, chan, lon_count = grid.shape
    m_dev = legendre.shape[0]
    n_wide = lax.axis_size("wide")
    rest = lat_dev - SUB
    fits = (
        lax.axis_size("narrow") == 2
        and chan == LANES
        and lon_count % 32 == 0
        and rest > 0
        and rest * m_dev == SUB
        and lat_dev % 2 == 0
        and n_wide % 16 == 0
        and lon_count * lon_count < 2**24
    )
    body = fast_shards if fits else general_shards
    return body(grid, quad_weights, orders, legendre, mix_real, mix_imag, filter_gain)


def solution(mesh):
    placed = (P("wide", "narrow", None), P("wide"), P(), P("wide", None, None), P(), P(), P())
    return jax.shard_map(
        shards, mesh=mesh, in_specs=placed, out_specs=P("wide", "narrow", None), check_vma=False
    )
```

```python
import functools
import math

import jax
import jax.numpy as jnp
from jax import lax
from jax.experimental import pallas as pl
from jax.experimental.pallas import tpu as pltpu
from jax.sharding import PartitionSpec as P

MESH = pl.DeviceIdType.MESH
SUB = 8
LANES = 128


def fourier_tables(orders, lon_count):
    columns = jnp.arange(lon_count, dtype=jnp.int32)
    phase_int = orders[:, None] * columns[None, :] % lon_count
    angles = phase_int.astype(jnp.float32) * (2.0 * math.pi / lon_count)
    return (jnp.cos(angles).astype(jnp.bfloat16), jnp.sin(angles).astype(jnp.bfloat16))


def general_shards(grid, quad_weights, orders, legendre, mix_real, mix_imag, filter_gain):
    lon_count = grid.shape[2]
    order_count = orders.shape[0]
    cosine_table, sine_table = fourier_tables(orders, lon_count)
    factor = 1.0 / math.sqrt(lon_count)
    real_part = (
        jnp.einsum("acn,kn->kac", grid, cosine_table, preferred_element_type=jnp.float32) * factor
    )
    imag_part = (
        -jnp.einsum("acn,kn->kac", grid, sine_table, preferred_element_type=jnp.float32) * factor
    )
    spectra = (
        jnp.stack([real_part, imag_part], axis=2) * quad_weights[None, :, None, None]
    ).astype(jnp.bfloat16)
    by_order = lax.all_to_all(spectra, "wide", split_axis=0, concat_axis=1, tiled=True)
    m_dev = by_order.shape[0]
    lat_count = by_order.shape[1]
    chan_dev = by_order.shape[3]
    deg_count = legendre.shape[1]
    coeffs = jnp.einsum(
        "mlx,mxk->mlk",
        legendre,
        by_order.reshape(m_dev, lat_count, 2 * chan_dev),
        preferred_element_type=jnp.float32,
    )
    coeffs = coeffs.astype(jnp.bfloat16).reshape(m_dev, deg_count, 2, chan_dev)
    deg_dev = deg_count // lax.axis_size("narrow")
    gain_rows = lax.dynamic_slice_in_dim(
        filter_gain, lax.axis_index("narrow") * deg_dev, deg_dev, 0
    ).astype(jnp.float32)
    upper = jnp.concatenate([mix_real, mix_imag], axis=1)
    lower = jnp.concatenate([-mix_imag, mix_real], axis=1)
    wide_block = jnp.concatenate([upper, lower], axis=0)
    fragment = lax.all_to_all(coeffs, "narrow", split_axis=1, concat_axis=3, tiled=True)
    frag_count = fragment.shape[0]
    chan_all = fragment.shape[3]
    flat_rows = fragment.reshape(frag_count * deg_dev, 2 * chan_all)
    product = jnp.dot(flat_rows, wide_block, preferred_element_type=jnp.float32)
    product = product.reshape(frag_count, deg_dev, 2, chan_all) * gain_rows[None, :, None, :]
    mixed_coeffs = product.astype(jnp.bfloat16)
    back_coeffs = lax.all_to_all(mixed_coeffs, "narrow", split_axis=3, concat_axis=1, tiled=True)
    synthesis = jnp.einsum(
        "mlx,mlk->mxk",
        legendre,
        back_coeffs.reshape(m_dev, deg_count, 2 * chan_dev),
        preferred_element_type=jnp.float32,
    )
    synthesis = synthesis.astype(jnp.bfloat16).reshape(m_dev, lat_count, 2, chan_dev)
    by_latitude = lax.all_to_all(synthesis, "wide", split_axis=1, concat_axis=0, tiled=True)
    field_out = jnp.einsum(
        "kac,kn->acn", by_latitude[:, :, 0], cosine_table, preferred_element_type=jnp.float32
    )
    field_out = field_out - jnp.einsum(
        "kac,kn->acn", by_latitude[:, :, 1], sine_table, preferred_element_type=jnp.float32
    )
    return (field_out / math.sqrt(order_count)).astype(jnp.bfloat16)


def turn_cosine(phase, period):
    quarter = period // 4
    turns = jnp.floor(phase * (1.0 / quarter) + 0.5)
    angle = (phase - turns * quarter) * (2.0 * math.pi / period)
    quadrant = turns - 4.0 * jnp.floor(turns * 0.25)
    sq = angle * angle
    cosine = 1.0 + sq * (-0.5 + sq * (1.0 / 24 + sq * (-1.0 / 720 + sq * (1.0 / 40320))))
    sine = angle * (1.0 + sq * (-1.0 / 6 + sq * (1.0 / 120 + sq * (-1.0 / 5040 + sq * (1.0 / 362880)))))
    odd = (quadrant == 1.0) | (quadrant == 3.0)
    flip = (quadrant == 1.0) | (quadrant == 2.0)
    value = jnp.where(odd, sine, cosine)
    return jnp.where(flip, -value, value)


def spectral_kernel(
    dims, orders_hbm, quad_hbm, grid_hbm, leg_hbm, mixr_hbm, mixi_hbm, gain_hbm,
    out_ref, tabt_ref,
    grid_v, leg_v, mixr_v, mixi_v, gain_v, tab, spread_a, spread_b, send1, recv1, lt, lf,
    weight, mixed, send2, recv2, flat2, orders_ref, quad_ref,
    grid_sem, in_sem, local_sem, s_send, s_recv, f_send, f_recv, b_send, b_recv,
):
    n_wide, lat_dev, lon_count, chan, m_dev, deg_count = dims
    order_count = n_wide * m_dev
    rows = 2 * order_count
    rest = lat_dev - SUB
    parts = m_dev + 1
    half = n_wide * SUB
    pairs = lat_dev // 2
    me = lax.axis_index("wide")
    x = lax.axis_index("narrow")
    partner = 1 - x

    scalar_copies = []
    for i, (src, dst) in enumerate(((orders_hbm, orders_ref), (quad_hbm, quad_ref))):
        copy = pltpu.make_async_copy(src, dst, in_sem.at[4 + i])
        copy.start()
        scalar_copies.append(copy)
    grid_copies = []
    for p in range(pairs):
        copy = pltpu.make_async_copy(
            grid_hbm.at[pl.ds(2 * p, 2)], grid_v.at[pl.ds(2 * p, 2)], grid_sem.at[p]
        )
        copy.start()
        grid_copies.append(copy)
    in_copies = []
    for i, (src, dst) in enumerate(
        ((leg_hbm, leg_v), (mixr_hbm, mixr_v), (mixi_hbm, mixi_v), (gain_hbm, gain_v))
    ):
        copy = pltpu.make_async_copy(src, dst, in_sem.at[i])
        copy.start()
        in_copies.append(copy)

    barrier = pltpu.get_barrier_semaphore()
    for d in range(1, n_wide):
        pl.semaphore_signal(
            barrier, inc=1, device_id=((me + d) % n_wide, x), device_id_type=MESH
        )
    pl.semaphore_signal(barrier, inc=1, device_id=(me, partner), device_id_type=MESH)

    for copy in scalar_copies:
        copy.wait()
    row = lax.broadcasted_iota(jnp.int32, (rows, LANES), 0)
    lane = lax.broadcasted_iota(jnp.int32, (rows, LANES), 1)
    block_rows = 2 * n_wide
    order_row = jnp.zeros((rows, LANES), jnp.int32)
    for j in range(m_dev):
        for w in range(n_wide):
            slot = orders_ref[w * m_dev + j]
            hit = (row == j * block_rows + w) | (row == j * block_rows + n_wide + w)
            order_row = jnp.where(hit, slot, order_row)
    shift = jnp.zeros((rows, LANES), jnp.int32)
    for j in range(m_dev):
        low = j * block_rows + n_wide
        shift = jnp.where((row >= low) & (row < low + n_wide), lon_count // 4, shift)
    for start in range(0, lon_count, LANES):
        size = min(LANES, lon_count - start)
        phase = (order_row * (lane + start) + shift).astype(jnp.float32)
        value = turn_cosine(phase, lon_count)
        tab[:, start:start + size] = value.astype(jnp.bfloat16)[:, :size]
        tabt_ref[start:start + size, :] = jnp.transpose(value)[:size].astype(jnp.bfloat16)

    factor = 1.0 / math.sqrt(lon_count)

    def transform(p):
        grid_copies[p].wait()
        rhs = jnp.concatenate([grid_v[2 * p], grid_v[2 * p + 1]], axis=1)
        res = jnp.dot(tab[...], rhs, preferred_element_type=jnp.float32)
        for i in range(2):
            a = 2 * p + i
            part = res[:, i * chan:(i + 1) * chan] * (quad_ref[a] * factor)
            if a < SUB:
                spread_a[a * rows:(a + 1) * rows, :] = part
            else:
                for j in range(m_dev):
                    at = (j * rest + a - SUB) * block_rows
                    spread_b[at:at + block_rows, :] = part[j * block_rows:(j + 1) * block_rows]

    def wide_copy(part, d):
        to = (me + d) % n_wide
        where = pl.ds(0, m_dev) if part == 0 else pl.ds(m_dev, 1)
        return pltpu.make_async_remote_copy(
            src_ref=send1.at[to, where],
            dst_ref=recv1.at[0, me, where],
            send_sem=s_send.at[part, d],
            recv_sem=s_recv.at[part, me],
            device_id=(to, x),
            device_id_type=MESH,
        )

    def wide_arrival(part, src):
        where = pl.ds(0, m_dev) if part == 0 else pl.ds(m_dev, 1)
        return pltpu.make_async_remote_copy(
            src_ref=send1.at[src, where],
            dst_ref=recv1.at[0, src, where],
            send_sem=s_send.at[part, 0],
            recv_sem=s_recv.at[part, src],
            device_id=(src, x),
            device_id_type=MESH,
        )

    def forward_copy(part, src):
        where = pl.ds(0, m_dev) if part == 0 else pl.ds(m_dev, 1)
        return pltpu.make_async_remote_copy(
            src_ref=recv1.at[0, src, where],
            dst_ref=recv1.at[1, src, where],
            send_sem=f_send.at[part, src],
            recv_sem=f_recv.at[part, src],
            device_id=(me, partner),
            device_id_type=MESH,
        )

    def own_copy(part):
        where = pl.ds(0, m_dev) if part == 0 else pl.ds(m_dev, 1)
        return pltpu.make_async_copy(
            send1.at[me, where], recv1.at[0, me, where], local_sem.at[part]
        )

    for p in range(SUB // 2):
        transform(p)
    for w in range(n_wide):
        for j in range(m_dev):
            for ri in range(2):
                at = j * block_rows + ri * n_wide + w
                send1[w, j, :, ri * chan:(ri + 1) * chan] = spread_a[
                    pl.ds(at, SUB, stride=rows), :
                ].astype(jnp.bfloat16)
    pl.semaphore_wait(barrier, n_wide)
    for d in range(1, n_wide):
        wide_copy(0, d).start()
    own_copy(0).start()

    for p in range(SUB // 2, pairs):
        transform(p)
    for w in range(n_wide):
        for ri in range(2):
            send1[w, m_dev, :, ri * chan:(ri + 1) * chan] = spread_b[
                pl.ds(ri * n_wide + w, SUB, stride=block_rows), :
            ].astype(jnp.bfloat16)
    for d in range(1, n_wide):
        wide_copy(1, d).start()
    own_copy(1).start()
    for part in range(2):
        own_copy(part).wait()
        forward_copy(part, me).start()

    for copy in in_copies:
        copy.wait()
    lat_count = n_wide * lat_dev
    slot = lax.broadcasted_iota(jnp.int32, (2 * half, lat_count), 0)
    lat = lax.broadcasted_iota(jnp.int32, (2 * half, lat_count), 1)
    local = slot % SUB
    device = jnp.where(slot < half, slot, slot - half) // SUB
    for j in range(m_dev):
        tail = jnp.where(
            (local >= j * rest) & (local < (j + 1) * rest),
            device * lat_dev + SUB + local - j * rest,
            -1,
        )
        want = jnp.where(slot < half, device * lat_dev + local, tail)
        pick = (want == lat).astype(jnp.bfloat16)
        moved = jnp.dot(pick, leg_v[j], preferred_element_type=jnp.float32)
        lt[j] = moved.astype(jnp.bfloat16)
        lf[j] = jnp.transpose(moved).astype(jnp.bfloat16)
    own_cols = pl.ds(pl.multiple_of(x * chan, chan), chan)
    for i, who in enumerate((x, partner)):
        in_rows = pl.ds(pl.multiple_of(who * chan, chan), chan)
        re = mixr_v[in_rows, own_cols]
        im = mixi_v[in_rows, own_cols]
        top = 2 * i * chan
        weight[top:top + chan, :chan] = re
        weight[top:top + chan, chan:] = im
        weight[top + chan:top + 2 * chan, :chan] = -im
        weight[top + chan:top + 2 * chan, chan:] = re

    for part in range(2):
        for d in range(1, n_wide):
            src = (me + n_wide - d) % n_wide
            wide_arrival(part, src).wait_recv()
            forward_copy(part, src).start()
    for part in range(2):
        for d in range(n_wide):
            forward_copy(part, (me + n_wide - d) % n_wide).wait_recv()

    gain = gain_v[:, own_cols].astype(jnp.float32)
    gain = jnp.concatenate([gain, gain], axis=1)
    tails = []
    for j in range(m_dev):
        sides = []
        for side in range(2):
            head = recv1[side, :, j].reshape(half, 2 * chan)
            tail = recv1[side, :, m_dev].reshape(half, 2 * chan)
            sides.append(jnp.concatenate([head, tail], axis=0))
        spec = jnp.concatenate(sides, axis=1)
        coeffs = jnp.dot(lf[j], spec, preferred_element_type=jnp.float32).astype(jnp.bfloat16)
        product = jnp.dot(coeffs, weight[...], preferred_element_type=jnp.float32)
        mixed[j] = (product * gain).astype(jnp.bfloat16)
        syn = jnp.dot(lt[j], mixed[j], preferred_element_type=jnp.float32)
        send2[:, j] = syn[:half].astype(jnp.bfloat16).reshape(n_wide, SUB, 2 * chan)
        tails.append(syn[half:])
    total = functools.reduce(lambda a, b: a + b, tails)
    send2[:, m_dev] = total.astype(jnp.bfloat16).reshape(n_wide, SUB, 2 * chan)

    def back_copy(to, d):
        return pltpu.make_async_remote_copy(
            src_ref=send2.at[to],
            dst_ref=recv2.at[me],
            send_sem=b_send.at[d],
            recv_sem=b_recv.at[me],
            device_id=(to, x),
            device_id_type=MESH,
        )

    def back_arrival(src):
        return pltpu.make_async_remote_copy(
            src_ref=send2.at[src],
            dst_ref=recv2.at[src],
            send_sem=b_send.at[0],
            recv_sem=b_recv.at[src],
            device_id=(src, x),
            device_id_type=MESH,
        )

    for d in range(1, n_wide):
        back_copy((me + d) % n_wide, d).start()
    own_back = pltpu.make_async_copy(send2.at[me], recv2.at[me], local_sem.at[2])
    own_back.start()
    for part in range(2):
        for d in range(1, n_wide):
            wide_copy(part, d).wait_send()
        for d in range(n_wide):
            forward_copy(part, (me + n_wide - d) % n_wide).wait_send()
    own_back.wait()
    for d in range(1, n_wide):
        back_arrival((me + n_wide - d) % n_wide).wait_recv()
    for ri in range(2):
        flat2[ri] = recv2[:, :, :, ri * chan:(ri + 1) * chan].astype(jnp.float32).reshape(
            n_wide * parts * SUB, chan
        )
    for a in range(lat_dev):
        for j in range(m_dev):
            for ri in range(2):
                at = j * SUB + a if a < SUB else m_dev * SUB + j * rest + a - SUB
                top = j * block_rows + ri * n_wide
                out_ref[a, top:top + n_wide, :] = flat2[
                    ri, pl.ds(at, n_wide, stride=parts * SUB), :
                ].astype(jnp.bfloat16)
    for d in range(1, n_wide):
        back_copy((me + d) % n_wide, d).wait_send()


def field_kernel(scale, tabt_ref, syn_ref, out_hbm, held, sem):
    lat_dev, _, chan = held.shape
    copies = []
    for p in range(lat_dev // 2):
        rhs = jnp.concatenate([syn_ref[2 * p], syn_ref[2 * p + 1]], axis=1)
        res = jnp.dot(tabt_ref[...], rhs, preferred_element_type=jnp.float32) * scale
        res = res.astype(jnp.bfloat16)
        held[2 * p] = res[:, :chan]
        held[2 * p + 1] = res[:, chan:]
        both = pl.ds(2 * p, 2)
        copy = pltpu.make_async_copy(held.at[both], out_hbm.at[both], sem.at[p])
        copy.start()
        copies.append(copy)
    for copy in copies:
        copy.wait()


def fast_shards(grid, quad_weights, orders, legendre, mix_real, mix_imag, filter_gain):
    lat_dev, chan, lon_count = grid.shape
    order_count = orders.shape[0]
    m_dev, deg_count, lat_count = legendre.shape
    n_wide = lax.axis_size("wide")
    rows = 2 * order_count
    parts = m_dev + 1
    half = n_wide * SUB
    bf16, f32 = jnp.bfloat16, jnp.float32
    vmem = pl.BlockSpec(memory_space=pltpu.VMEM)
    hbm = pl.BlockSpec(memory_space=pltpu.HBM)
    dims = (n_wide, lat_dev, lon_count, chan, m_dev, deg_count)
    chan_all = mix_real.shape[0]
    dma = pltpu.SemaphoreType.DMA
    synthesis, table = pl.pallas_call(
        functools.partial(spectral_kernel, dims),
        out_shape=(
            jax.ShapeDtypeStruct((lat_dev, rows, chan), bf16),
            jax.ShapeDtypeStruct((lon_count, rows), bf16),
        ),
        in_specs=[hbm] * 7,
        out_specs=(vmem, vmem),
        scratch_shapes=[
            pltpu.VMEM((lat_dev, lon_count, chan), bf16),
            pltpu.VMEM((m_dev, lat_count, deg_count), bf16),
            pltpu.VMEM((chan_all, chan_all), bf16),
            pltpu.VMEM((chan_all, chan_all), bf16),
            pltpu.VMEM((deg_count, chan_all), bf16),
            pltpu.VMEM((rows, lon_count), bf16),
            pltpu.VMEM((SUB * rows, chan), f32),
            pltpu.VMEM(((lat_dev - SUB) * rows, chan), f32),
            pltpu.VMEM((n_wide, parts, SUB, 2 * chan), bf16),
            pltpu.VMEM((2, n_wide, parts, SUB, 2 * chan), bf16),
            pltpu.VMEM((m_dev, 2 * half, deg_count), bf16),
            pltpu.VMEM((m_dev, deg_count, 2 * half), bf16),
            pltpu.VMEM((4 * chan, 2 * chan), bf16),
            pltpu.VMEM((m_dev, deg_count, 2 * chan), bf16),
            pltpu.VMEM((n_wide, parts, SUB, 2 * chan), bf16),
            pltpu.VMEM((n_wide, parts, SUB, 2 * chan), bf16),
            pltpu.VMEM((2, n_wide * parts * SUB, chan), f32),
            pltpu.SMEM((order_count,), jnp.int32),
            pltpu.SMEM((lat_dev,), f32),
            dma((lat_dev // 2,)),
            dma((6,)),
            dma((3,)),
            dma((2, n_wide)),
            dma((2, n_wide)),
            dma((2, n_wide)),
            dma((2, n_wide)),
            dma((n_wide,)),
            dma((n_wide,)),
        ],
        compiler_params=pltpu.CompilerParams(
            collective_id=0, has_side_effects=True, vmem_limit_bytes=40 * 2**20
        ),
        name="spectral",
    )(*(pltpu.with_memory_space_constraint(v, pltpu.HBM) for v in (
        orders, quad_weights, jnp.transpose(grid, (0, 2, 1)), jnp.transpose(legendre, (0, 2, 1)),
        mix_real, mix_imag, filter_gain,
    )))
    field = pl.pallas_call(
        functools.partial(field_kernel, 1.0 / math.sqrt(order_count)),
        out_shape=jax.ShapeDtypeStruct((lat_dev, lon_count, chan), bf16),
        in_specs=[vmem, vmem],
        out_specs=pl.BlockSpec(memory_space=pl.ANY),
        scratch_shapes=[pltpu.VMEM((lat_dev, lon_count, chan), bf16), dma((lat_dev // 2,))],
        compiler_params=pltpu.CompilerParams(vmem_limit_bytes=24 * 2**20),
        name="field",
    )(table, synthesis)
    return jnp.transpose(field, (0, 2, 1))


def shards(grid, quad_weights, orders, legendre, mix_real, mix_imag, filter_gain):
    lat_dev, chan, lon_count = grid.shape
    m_dev = legendre.shape[0]
    n_wide = lax.axis_size("wide")
    rest = lat_dev - SUB
    fits = (
        lax.axis_size("narrow") == 2
        and chan == LANES
        and lon_count % 4 == 0
        and rest > 0
        and rest * m_dev == SUB
        and lat_dev % 2 == 0
        and n_wide % 16 == 0
        and lon_count * lon_count < 2**24
    )
    body = fast_shards if fits else general_shards
    return body(grid, quad_weights, orders, legendre, mix_real, mix_imag, filter_gain)


def solution(mesh):
    placed = (P("wide", "narrow", None), P("wide"), P(), P("wide", None, None), P(), P(), P())
    return jax.shard_map(
        shards, mesh=mesh, in_specs=placed, out_specs=P("wide", "narrow", None), check_vma=False
    )
```
